32 devices in a mesh: group: 2 (over x), cand: 16 (over z, y, core).
Axes of the slice: x: 2, y: 2, z: 4, core: 2. Of those that a mesh axis runs over, the one named last changes fastest.
Arguments:
- embeddings: bfloat16 [64, 1024, 768], P(('group', 'cand')), parts along dimension 0
- lengths: int32 [64], P(('group', 'cand')), parts along dimension 0, may hold values from 256 to 1024, as said below
Outputs:
- consensus: float32 [64, 1024], P(('group', 'cand')), parts along dimension 0
The draws below stay inside these ranges and needn't reach their ends.
There are 2 independent parts, one for each index of `group`. The reference program is written for one: setup_inputs(seed, part) draws one part's arguments, and reference() takes and returns one part's arrays. A program takes and returns all parts, laid end to end along the dimension named above; each array names one. Nothing has to cross between parts.
Inputs may be any that keep to these rules, and one draw needn't show every extreme that they name: `lengths`: at least one answer of every prompt has exactly 1024 tokens; every answer has 256 tokens or more.
All inputs are finite; a program needn't handle non-finite values.
Results may differ from the reference program's by a relative error of at most 0.0005.
Values may be sent and summed in bfloat16 or wider, within the bound.
A program may use at most 64 MiB of HBM per device.

```python
import jax
import jax.numpy as jnp
from jax import lax

A_DEV = 2
L = 1024
E = 768
ROUNDS = 2
CAND = 32
PARTNERS = 9
N_CAND = 16


def draw_embeddings(key, part):
    key_base = jax.random.fold_in(key, 11)
    base = jax.random.normal(key_base, (CAND, L, E), jnp.float32)
    return base.astype(jnp.bfloat16)


def draw_lengths(key, part):
    drawn = jax.random.randint(jax.random.fold_in(key, 21), (CAND,), L // 4, L + 1)
    where_full = jax.random.randint(jax.random.fold_in(key, 22), (), 0, CAND)
    return drawn.at[where_full].set(L).astype(jnp.int32)


def setup_inputs(seed: int = 0, part: int = 0) -> dict:
    streams_of = jax.random.split(jax.random.key(seed), 3)
    own_keys = jax.random.split(jax.random.fold_in(streams_of[2], part), 3)
    return {
        "embeddings": draw_embeddings(jax.random.fold_in(jax.random.fold_in(streams_of[2], part), 71), part),
        "lengths": draw_lengths(jax.random.fold_in(jax.random.fold_in(streams_of[2], part), 71), part),
    }


INV_TEMP = 256.0

def unit_rows(embeddings):
    values = embeddings.astype(jnp.float32)
    scale = lax.rsqrt(lax.optimization_barrier(jnp.sum(values * values, axis=-1, keepdims=True)) + 1e-06)
    return (values * scale).astype(jnp.bfloat16)

def soft_terms(left, left_valid, right, right_valid):
    scores = jnp.einsum('te,bse->bts', left.astype(jnp.float32), right.astype(jnp.float32)) * INV_TEMP
    row_scores = jnp.where(right_valid[:, None, :] > 0.5, scores, -1e+30)
    row_peak = lax.optimization_barrier(jnp.max(row_scores, axis=2, keepdims=True))
    row_terms = (row_peak[..., 0] + jnp.log(lax.optimization_barrier(jnp.sum(jnp.exp(row_scores - row_peak), axis=2)))) / INV_TEMP
    col_scores = jnp.where(left_valid[None, :, None] > 0.5, scores, -1e+30)
    col_peak = lax.optimization_barrier(jnp.max(col_scores, axis=1, keepdims=True))
    col_terms = (col_peak[:, 0, :] + jnp.log(lax.optimization_barrier(jnp.sum(jnp.exp(col_scores - col_peak), axis=1)))) / INV_TEMP
    return (row_terms, col_terms)

def reference(embeddings, lengths):
    unit = unit_rows(embeddings)
    valid = (jnp.arange(L, dtype=jnp.int32)[None, :] < lengths[:, None]).astype(jnp.float32)

    def visit(totals, index):
        block = index // A_DEV
        start = (block * A_DEV).astype(jnp.int32)
        mine = unit[index]
        mine_valid = valid[index]
        same = lax.dynamic_slice_in_dim(unit, start, A_DEV, 0)
        same_valid = lax.dynamic_slice_in_dim(valid, start, A_DEV, 0)
        row_terms, unused = soft_terms(mine, mine_valid, same, same_valid)
        weight = (jnp.arange(A_DEV, dtype=jnp.int32) + start != index).astype(jnp.float32)
        own_sum = lax.optimization_barrier(jnp.sum(row_terms * weight[:, None], axis=0))
        for offset in range(1, ROUNDS + 1):
            other = ((block - offset) % N_CAND * A_DEV).astype(jnp.int32)
            theirs = lax.dynamic_slice_in_dim(unit, other, A_DEV, 0)
            their_valid = lax.dynamic_slice_in_dim(valid, other, A_DEV, 0)
            row_terms, col_terms = soft_terms(mine, mine_valid, theirs, their_valid)
            own_sum = own_sum + lax.optimization_barrier(jnp.sum(row_terms, axis=0))
            current = lax.dynamic_slice_in_dim(totals, other, A_DEV, 0)
            totals = lax.dynamic_update_slice_in_dim(totals, current + col_terms, other, 0)
        totals = totals.at[index].add(own_sum)
        return (totals, None)
    totals, unused = lax.scan(visit, jnp.zeros((CAND, L), jnp.float32), jnp.arange(CAND, dtype=jnp.int32))
    return totals * valid / PARTNERS
```

```python
import functools
import math

import jax
import jax.numpy as jnp
from jax import lax
from jax.experimental import pallas as pl
from jax.experimental.pallas import tpu as pltpu
from jax.sharding import PartitionSpec as P

MESH = pl.DeviceIdType.MESH
INV_TEMP = 256.0
LOW = -1e30
ROWS = 128


def unit_rows(raw):
    values = raw.astype(jnp.float32)
    scale = lax.rsqrt(jnp.sum(values * values, axis=-1, keepdims=True) + 1e-06)
    return (values * scale).astype(jnp.bfloat16)


def kernel(
    n, x_hbm, lens_ref, out_ref,
    raw, units, fresh, lens, bias, peak, mass, total, back,
    local_sem, send_sem, recv_sem,
):
    answers, length = x_hbm.shape[0], x_hbm.shape[1]
    chunks = length // ROWS
    me = lax.axis_index("cand")
    parity = lax.rem(me, 2)
    partner = me + 1 - 2 * parity
    other = lax.rem(me + n - 1 + 2 * parity, n)

    barrier = pltpu.get_barrier_semaphore()
    for device in (partner, other):
        pl.semaphore_signal(barrier, inc=1, device_id={"cand": device}, device_id_type=MESH)
    local = pltpu.make_async_copy(x_hbm, raw.at[0], local_sem)
    local.start()
    pl.semaphore_wait(barrier, 2)

    def remote(src, dst, sem, device):
        return pltpu.make_async_remote_copy(
            src_ref=src, dst_ref=dst, send_sem=send_sem.at[sem], recv_sem=recv_sem.at[sem],
            device_id={"cand": device}, device_id_type=MESH,
        )

    def piece(k):
        rows = pl.ds(pl.multiple_of(k * ROWS, ROWS), ROWS)
        return remote(x_hbm.at[:, rows], raw.at[2, :, rows], k, other)

    lens_c = remote(lens_ref, lens.at[1], chunks, partner)
    lens_r = remote(lens_ref, lens.at[2], chunks + 1, other)
    block_c = remote(x_hbm, raw.at[1], chunks + 2, partner)
    lens_r.start()
    lens_c.start()
    for k in range(chunks):
        piece(k).start()
        if k == 0:
            block_c.start()

    lane = lax.broadcasted_iota(jnp.int32, (1, length), 1)
    eye = lax.broadcasted_iota(jnp.int32, (ROWS, ROWS), 0) == lax.broadcasted_iota(
        jnp.int32, (ROWS, ROWS), 1
    )
    total[...] = jnp.zeros_like(total)
    peak[...] = jnp.full_like(peak, LOW)
    mass[...] = jnp.zeros_like(mass)

    def set_bias(slot, counts):
        for a in range(answers):
            bias[slot * answers + a] = jnp.where(lane < counts[a : a + 1, 0:1], 0.0, LOW)

    def normalise(slot):
        def one(i, carry):
            a, k = i // chunks, lax.rem(i, chunks)
            rows = pl.ds(pl.multiple_of(k * ROWS, ROWS), ROWS)
            units[slot * answers + a, rows] = unit_rows(raw[slot, a, rows])
            return carry

        lax.fori_loop(0, answers * chunks, one, 0)

    def tile(query, row_slot, k, left, pair):
        cols = pl.ds(pl.multiple_of(k * ROWS, ROWS), ROWS)
        row_bias = jnp.broadcast_to(bias[row_slot, :, cols], (ROWS, ROWS))
        row_bias = jnp.sum(jnp.where(eye, row_bias, 0.0), axis=1, keepdims=True)
        scores = lax.dot_general(
            query, units[left], (((1,), (1,)), ((), ())), preferred_element_type=jnp.float32
        )
        scores = scores * (INV_TEMP / math.log(2.0)) + bias[left] + row_bias
        top = jnp.max(scores, axis=1, keepdims=True)
        row_sum = jnp.sum(jnp.exp2(scores - top), axis=1, keepdims=True)
        term = (top + jnp.log2(row_sum)) * (math.log(2.0) / INV_TEMP)
        term = jnp.sum(jnp.where(eye, jnp.broadcast_to(term, (ROWS, ROWS)), 0.0), axis=0, keepdims=True)
        total[row_slot, :, cols] = total[row_slot, :, cols] + term
        before = peak[pair]
        now = jnp.maximum(before, jnp.max(scores, axis=0, keepdims=True))
        peak[pair] = now
        mass[pair] = mass[pair] * jnp.exp2(before - now) + jnp.sum(
            jnp.exp2(scores - now), axis=0, keepdims=True
        )

    def close(left, pair):
        total[left] = total[left] + (peak[pair] + jnp.log2(mass[pair])) * (
            math.log(2.0) / INV_TEMP
        )

    local.wait()
    set_bias(0, lens_ref[...])
    normalise(0)

    def own(k, carry):
        rows = pl.ds(pl.multiple_of(k * ROWS, ROWS), ROWS)
        tile(units[1, rows], 1, k, 0, 0)
        return carry

    lax.fori_loop(0, chunks, own, 0)
    close(0, 0)

    lens_c.wait()
    block_c.wait()
    set_bias(1, lens[1])
    normalise(1)

    def near(i, carry):
        a, k = i // chunks, lax.rem(i, chunks)
        rows = pl.ds(pl.multiple_of(k * ROWS, ROWS), ROWS)
        slot = answers + lax.rem(a + parity, 2)
        tile(units[slot, rows], slot, k, a, 1 + a)
        return carry

    lax.fori_loop(0, answers * chunks, near, 0)
    for a in range(answers):
        close(a, 1 + a)

    lens_r.wait()
    set_bias(2, lens[2])
    first = 1 + answers

    def far(k, carry):
        piece(k).wait()
        rows = pl.ds(pl.multiple_of(k * ROWS, ROWS), ROWS)
        for b in range(answers):
            fresh[b] = unit_rows(raw[2, b, rows])

        def one(p, carry):
            cross = p < answers * answers
            left = jnp.where(cross, answers + p // answers, p - answers * answers)
            b = jnp.where(cross, lax.rem(p, answers), lax.rem(left + parity, 2))
            tile(fresh[b], 2 * answers + b, k, left, first + p)
            return carry

        lax.fori_loop(0, answers * answers + answers, one, 0)
        return carry

    lax.fori_loop(0, chunks, far, 0)

    back_r = remote(total.at[pl.ds(2 * answers, answers)], back.at[1], chunks + 3, other)
    back_c = remote(total.at[pl.ds(answers, answers)], back.at[0], chunks + 4, partner)
    back_r.start()
    for p in range(answers * answers):
        close(answers + p // answers, first + p)
    back_c.start()
    for a in range(answers):
        close(a, first + answers * answers + a)
    back_c.wait()
    back_r.wait()
    for a in range(answers):
        whole = total[a] + back[0, a] + back[1, a]
        out_ref[a : a + 1] = jnp.where(bias[a] == 0.0, whole / (answers - 1 + 4 * answers), 0.0)


def solution(mesh):
    n = mesh.shape["cand"]

    def shards(embeddings, lengths):
        answers, length, width = embeddings.shape
        chunks = length // ROWS
        pairs = 1 + 2 * answers + answers * answers
        counts = jnp.broadcast_to(lengths[:, None], (answers, 128))
        counts = jnp.pad(counts, ((0, 8 - answers), (0, 0)))
        return pl.pallas_call(
            functools.partial(kernel, n),
            out_shape=jax.ShapeDtypeStruct((answers, length), jnp.float32),
            in_specs=[
                pl.BlockSpec(memory_space=pl.ANY),
                pl.BlockSpec(memory_space=pltpu.VMEM),
            ],
            out_specs=pl.BlockSpec(memory_space=pltpu.VMEM),
            scratch_shapes=[
                pltpu.VMEM((3, answers, length, width), jnp.bfloat16),
                pltpu.VMEM((2 * answers, length, width), jnp.bfloat16),
                pltpu.VMEM((answers, ROWS, width), jnp.bfloat16),
                pltpu.VMEM((3, 8, 128), jnp.int32),
                pltpu.VMEM((3 * answers, 1, length), jnp.float32),
                pltpu.VMEM((pairs, 1, length), jnp.float32),
                pltpu.VMEM((pairs, 1, length), jnp.float32),
                pltpu.VMEM((3 * answers, 1, length), jnp.float32),
                pltpu.VMEM((2, answers, 1, length), jnp.float32),
                pltpu.SemaphoreType.DMA,
                pltpu.SemaphoreType.DMA((chunks + 5,)),
                pltpu.SemaphoreType.DMA((chunks + 5,)),
            ],
            compiler_params=pltpu.CompilerParams(collective_id=0, has_side_effects=True),
            name="consensus",
        )(embeddings, counts)

    return jax.shard_map(
        shards,
        mesh=mesh,
        in_specs=(P(("group", "cand"), None, None), P(("group", "cand"))),
        out_specs=P(("group", "cand"), None),
        check_vma=False,
    )
```

```python
import functools

import jax
import jax.numpy as jnp
from jax import lax
from jax.experimental import pallas as pl
from jax.experimental.pallas import tpu as pltpu
from jax.sharding import PartitionSpec as P

MESH = pl.DeviceIdType.MESH
INV_TEMP = 256.0
LOW = -1e30
ROWS = 128
WIDE = 256


def unit_rows(raw):
    values = raw.astype(jnp.float32)
    scale = lax.rsqrt(jnp.sum(values * values, axis=-1, keepdims=True) + 1e-06)
    return (values * scale).astype(jnp.bfloat16)


def kernel(
    n, x_hbm, lens_ref, out_ref,
    raw, units, across, fresh, board, lens, bias, peak, mass, total, back,
    local_sem, send_sem, recv_sem,
):
    answers, length = x_hbm.shape[0], x_hbm.shape[1]
    chunks = length // ROWS
    me = lax.axis_index("cand")
    parity = lax.rem(me, 2)
    partner = me + 1 - 2 * parity
    other = lax.rem(me + n - 1 + 2 * parity, n)

    barrier = pltpu.get_barrier_semaphore()
    for device in (partner, other):
        pl.semaphore_signal(barrier, inc=1, device_id={"cand": device}, device_id_type=MESH)
    local = pltpu.make_async_copy(x_hbm, raw.at[0], local_sem)
    local.start()
    pl.semaphore_wait(barrier, 2)

    def remote(src, dst, sem, device):
        return pltpu.make_async_remote_copy(
            src_ref=src, dst_ref=dst, send_sem=send_sem.at[sem], recv_sem=recv_sem.at[sem],
            device_id={"cand": device}, device_id_type=MESH,
        )

    def piece(k):
        rows = pl.ds(pl.multiple_of(k * ROWS, ROWS), ROWS)
        return remote(x_hbm.at[:, rows], raw.at[2, :, rows], k, other)

    lens_c = remote(lens_ref, lens.at[1], chunks, partner)
    lens_r = remote(lens_ref, lens.at[2], chunks + 1, other)
    block_c = remote(x_hbm, raw.at[1], chunks + 2, partner)
    lens_r.start()
    lens_c.start()
    for k in range(chunks):
        piece(k).start()
        if k == 0:
            block_c.start()

    lane = lax.broadcasted_iota(jnp.int32, (1, length), 1)
    eye = lax.broadcasted_iota(jnp.int32, (ROWS, ROWS), 0) == lax.broadcasted_iota(
        jnp.int32, (ROWS, ROWS), 1
    )
    total[...] = jnp.zeros_like(total)
    peak[...] = jnp.full_like(peak, LOW)
    mass[...] = jnp.zeros_like(mass)

    def set_bias(slot, counts):
        for a in range(answers):
            bias[slot * answers + a] = jnp.where(lane < counts[a : a + 1, 0:1], 0.0, LOW)

    def normalise(slot):
        def one(i, carry):
            a, k = i // chunks, lax.rem(i, chunks)
            rows = pl.ds(pl.multiple_of(k * ROWS, ROWS), ROWS)
            unit = unit_rows(raw[slot, a, rows])
            units[slot * answers + a, rows] = unit
            across[slot * answers + a, :, rows] = unit.T
            return carry

        lax.fori_loop(0, answers * chunks, one, 0)

    def score(query, left, place):
        for j in range(0, length, WIDE):
            board[pl.ds(place, query.shape[0]), j : j + WIDE] = INV_TEMP * lax.dot_general(
                query, across[left, :, j : j + WIDE], (((1,), (0,)), ((), ())),
                preferred_element_type=jnp.float32,
            ) + bias[left, :, j : j + WIDE]

    def fold(place, row_slot, k, pair):
        cols = pl.ds(pl.multiple_of(k * ROWS, ROWS), ROWS)
        row_bias = jnp.broadcast_to(bias[row_slot, :, cols], (ROWS, ROWS))
        row_bias = jnp.sum(jnp.where(eye, row_bias, 0.0), axis=1, keepdims=True)
        rows = pl.ds(place, ROWS)
        tops = None
        for j in range(0, length, WIDE):
            scores = board[rows, j : j + WIDE] + row_bias
            board[rows, j : j + WIDE] = scores
            before = peak[pair, :, j : j + WIDE]
            now = jnp.maximum(before, jnp.max(scores, axis=0, keepdims=True))
            peak[pair, :, j : j + WIDE] = now
            mass[pair, :, j : j + WIDE] = mass[pair, :, j : j + WIDE] * jnp.exp(
                before - now
            ) + jnp.sum(jnp.exp(scores - now), axis=0, keepdims=True)
            for i in range(0, WIDE, 128):
                part = scores[:, i : i + 128]
                tops = part if tops is None else jnp.maximum(tops, part)
        top = jnp.max(tops, axis=1, keepdims=True)
        sums = None
        for j in range(0, length, 128):
            part = jnp.exp(board[rows, j : j + 128] - top)
            sums = part if sums is None else sums + part
        term = (top + jnp.log(jnp.sum(sums, axis=1, keepdims=True))) / INV_TEMP
        term = jnp.sum(jnp.where(eye, jnp.broadcast_to(term, (ROWS, ROWS)), 0.0), axis=0, keepdims=True)
        total[row_slot, :, cols] = total[row_slot, :, cols] + term

    def close(left, pair):
        total[left] = total[left] + (peak[pair] + jnp.log(mass[pair])) / INV_TEMP

    local.wait()
    set_bias(0, lens_ref[...])
    normalise(0)

    def own(k, carry):
        rows = pl.ds(pl.multiple_of(k * (2 * ROWS), 2 * ROWS), 2 * ROWS)
        score(units[1, rows], 0, 0)
        for h in range(2):
            fold(h * ROWS, 1, 2 * k + h, 0)
        return carry

    lax.fori_loop(0, chunks // 2, own, 0)
    close(0, 0)

    lens_c.wait()
    block_c.wait()
    set_bias(1, lens[1])
    normalise(1)

    def near(k, carry):
        rows = pl.ds(pl.multiple_of(k * (2 * ROWS), 2 * ROWS), 2 * ROWS)
        for a in range(answers):
            slot = answers + lax.rem(a + parity, 2)
            score(units[slot, rows], a, a * 2 * ROWS)
        for a in range(answers):
            slot = answers + lax.rem(a + parity, 2)
            for h in range(2):
                fold((2 * a + h) * ROWS, slot, 2 * k + h, 1 + a)
        return carry

    lax.fori_loop(0, chunks // 2, near, 0)
    for a in range(answers):
        close(a, 1 + a)

    lens_r.wait()
    set_bias(2, lens[2])
    first = 1 + answers

    def far(k, carry):
        piece(k).wait()
        rows = pl.ds(pl.multiple_of(k * ROWS, ROWS), ROWS)
        for b in range(answers):
            fresh[pl.ds(b * ROWS, ROWS)] = unit_rows(raw[2, b, rows])
        for a in range(answers):
            score(fresh[...], answers + a, a * answers * ROWS)
        for a in range(answers):
            b = lax.rem(a + parity, 2)
            mine = fresh[pl.ds(pl.multiple_of(b * ROWS, ROWS), ROWS)]
            score(mine, a, (answers * answers + a) * ROWS)
        for a in range(answers):
            for b in range(answers):
                p = a * answers + b
                fold(p * ROWS, 2 * answers + b, k, first + p)
        for a in range(answers):
            p = answers * answers + a
            fold(p * ROWS, 2 * answers + lax.rem(a + parity, 2), k, first + p)
        return carry

    lax.fori_loop(0, chunks, far, 0)

    back_r = remote(total.at[pl.ds(2 * answers, answers)], back.at[1], chunks + 3, other)
    back_c = remote(total.at[pl.ds(answers, answers)], back.at[0], chunks + 4, partner)
    back_r.start()
    for p in range(answers * answers):
        close(answers + p // answers, first + p)
    back_c.start()
    for a in range(answers):
        close(a, first + answers * answers + a)
    back_c.wait()
    back_r.wait()
    for a in range(answers):
        whole = total[a] + back[0, a] + back[1, a]
        out_ref[a : a + 1] = jnp.where(bias[a] == 0.0, whole / (answers - 1 + 4 * answers), 0.0)


def solution(mesh):
    n = mesh.shape["cand"]

    def shards(embeddings, lengths):
        answers, length, width = embeddings.shape
        chunks = length // ROWS
        pairs = 1 + 2 * answers + answers * answers
        counts = jnp.broadcast_to(lengths[:, None], (answers, 128))
        counts = jnp.pad(counts, ((0, 8 - answers), (0, 0)))
        return pl.pallas_call(
            functools.partial(kernel, n),
            out_shape=jax.ShapeDtypeStruct((answers, length), jnp.float32),
            in_specs=[
                pl.BlockSpec(memory_space=pl.ANY),
                pl.BlockSpec(memory_space=pltpu.VMEM),
            ],
            out_specs=pl.BlockSpec(memory_space=pltpu.VMEM),
            scratch_shapes=[
                pltpu.VMEM((3, answers, length, width), jnp.bfloat16),
                pltpu.VMEM((2 * answers, length, width), jnp.bfloat16),
                pltpu.VMEM((2 * answers, width, length), jnp.bfloat16),
                pltpu.VMEM((answers * ROWS, width), jnp.bfloat16),
                pltpu.VMEM((answers * (answers + 1) * ROWS, length), jnp.float32),
                pltpu.VMEM((3, 8, 128), jnp.int32),
                pltpu.VMEM((3 * answers, 1, length), jnp.float32),
                pltpu.VMEM((pairs, 1, length), jnp.float32),
                pltpu.VMEM((pairs, 1, length), jnp.float32),
                pltpu.VMEM((3 * answers, 1, length), jnp.float32),
                pltpu.VMEM((2, answers, 1, length), jnp.float32),
                pltpu.SemaphoreType.DMA,
                pltpu.SemaphoreType.DMA((chunks + 5,)),
                pltpu.SemaphoreType.DMA((chunks + 5,)),
            ],
            compiler_params=pltpu.CompilerParams(collective_id=0, has_side_effects=True),
            name="consensus",
        )(embeddings, counts)

    return jax.shard_map(
        shards,
        mesh=mesh,
        in_specs=(P(("group", "cand"), None, None), P(("group", "cand"))),
        out_specs=P(("group", "cand"), None),
        check_vma=False,
    )
```

```python
import functools

import jax
import jax.numpy as jnp
from jax import lax
from jax.experimental import pallas as pl
from jax.experimental.pallas import tpu as pltpu
from jax.sharding import PartitionSpec as P

MESH = pl.DeviceIdType.MESH
INV_TEMP = 256.0
LOW = -1e30
ROWS = 128
WIDE = 256


def unit_rows(raw):
    values = raw.astype(jnp.float32)
    scale = lax.rsqrt(jnp.sum(values * values, axis=-1, keepdims=True) + 1e-06)
    return (values * scale).astype(jnp.bfloat16)


def kernel(
    n, x_hbm, lens_ref, out_ref,
    raw, units, across, fresh, board, lens, bias, peak, mass, total, back,
    local_sem, send_sem, recv_sem,
):
    answers, length = x_hbm.shape[0], x_hbm.shape[1]
    chunks = length // ROWS
    pieces = answers * chunks
    me = lax.axis_index("cand")
    parity = lax.rem(me, 2)
    partner = me + 1 - 2 * parity
    other = lax.rem(me + n - 1 + 2 * parity, n)

    for a in range(answers):
        lens[0, a : a + 1] = jnp.full((1, 128), lens_ref[a], jnp.int32)

    barrier = pltpu.get_barrier_semaphore()
    for device in (partner, other):
        pl.semaphore_signal(barrier, inc=1, device_id={"cand": device}, device_id_type=MESH)
    local = pltpu.make_async_copy(x_hbm, raw.at[0], local_sem)
    local.start()
    pl.semaphore_wait(barrier, 2)

    def remote(src, dst, sem, device):
        return pltpu.make_async_remote_copy(
            src_ref=src, dst_ref=dst, send_sem=send_sem.at[sem], recv_sem=recv_sem.at[sem],
            device_id={"cand": device}, device_id_type=MESH,
        )

    def piece(i):
        b, k = lax.rem(i, answers), i // answers
        rows = pl.ds(pl.multiple_of(k * ROWS, ROWS), ROWS)
        return remote(x_hbm.at[b, rows], raw.at[2, b, rows], i, other)

    lens_c = remote(lens.at[0], lens.at[1], pieces, partner)
    lens_r = remote(lens.at[0], lens.at[2], pieces + 1, other)
    block_c = remote(x_hbm, raw.at[1], pieces + 2, partner)
    lens_r.start()
    lens_c.start()
    block_c.start()

    def launch(i, carry):
        piece(i).start()
        return carry

    lax.fori_loop(0, pieces, launch, 0)

    lane = lax.broadcasted_iota(jnp.int32, (1, length), 1)
    eye = lax.broadcasted_iota(jnp.int32, (ROWS, ROWS), 0) == lax.broadcasted_iota(
        jnp.int32, (ROWS, ROWS), 1
    )
    total[...] = jnp.zeros_like(total)
    peak[...] = jnp.full_like(peak, LOW)
    mass[...] = jnp.zeros_like(mass)

    def set_bias(slot, counts):
        for a in range(answers):
            bias[slot * answers + a] = jnp.where(lane < counts[a : a + 1, 0:1], 0.0, LOW)

    def normalise(slot):
        def one(i, carry):
            a, k = i // chunks, lax.rem(i, chunks)
            rows = pl.ds(pl.multiple_of(k * ROWS, ROWS), ROWS)
            unit = unit_rows(raw[slot, a, rows])
            units[slot * answers + a, rows] = unit
            across[slot * answers + a, :, rows] = unit.T
            return carry

        lax.fori_loop(0, answers * chunks, one, 0)

    def score(query, left, place):
        for j in range(0, length, WIDE):
            board[pl.ds(place, query.shape[0]), j : j + WIDE] = INV_TEMP * lax.dot_general(
                query, across[left, :, j : j + WIDE], (((1,), (0,)), ((), ())),
                preferred_element_type=jnp.float32,
            ) + bias[left, :, j : j + WIDE]

    def fold(place, row_slot, k, pair):
        cols = pl.ds(pl.multiple_of(k * ROWS, ROWS), ROWS)
        row_bias = jnp.broadcast_to(bias[row_slot, :, cols], (ROWS, ROWS))
        row_bias = jnp.sum(jnp.where(eye, row_bias, 0.0), axis=1, keepdims=True)
        rows = pl.ds(place, ROWS)
        tops = None
        for j in range(0, length, WIDE):
            scores = board[rows, j : j + WIDE] + row_bias
            board[rows, j : j + WIDE] = scores
            before = peak[pair, :, j : j + WIDE]
            now = jnp.maximum(before, jnp.max(scores, axis=0, keepdims=True))
            peak[pair, :, j : j + WIDE] = now
            mass[pair, :, j : j + WIDE] = mass[pair, :, j : j + WIDE] * jnp.exp(
                before - now
            ) + jnp.sum(jnp.exp(scores - now), axis=0, keepdims=True)
            for i in range(0, WIDE, 128):
                part = scores[:, i : i + 128]
                tops = part if tops is None else jnp.maximum(tops, part)
        top = jnp.max(tops, axis=1, keepdims=True)
        sums = None
        for j in range(0, length, 128):
            part = jnp.exp(board[rows, j : j + 128] - top)
            sums = part if sums is None else sums + part
        term = (top + jnp.log(jnp.sum(sums, axis=1, keepdims=True))) / INV_TEMP
        term = jnp.sum(jnp.where(eye, jnp.broadcast_to(term, (ROWS, ROWS)), 0.0), axis=0, keepdims=True)
        total[row_slot, :, cols] = total[row_slot, :, cols] + term

    def close(left, pair):
        total[left] = total[left] + (peak[pair] + jnp.log(mass[pair])) / INV_TEMP

    local.wait()
    set_bias(0, lens[0])
    normalise(0)

    def own(k, carry):
        rows = pl.ds(pl.multiple_of(k * (2 * ROWS), 2 * ROWS), 2 * ROWS)
        score(units[1, rows], 0, 0)
        for h in range(2):
            fold(h * ROWS, 1, 2 * k + h, 0)
        return carry

    lax.fori_loop(0, chunks // 2, own, 0)
    close(0, 0)

    lens_c.wait()
    block_c.wait()
    set_bias(1, lens[1])
    normalise(1)

    def near(k, carry):
        rows = pl.ds(pl.multiple_of(k * (2 * ROWS), 2 * ROWS), 2 * ROWS)
        for a in range(answers):
            slot = answers + lax.rem(a + parity, 2)
            score(units[slot, rows], a, a * 2 * ROWS)
        for a in range(answers):
            slot = answers + lax.rem(a + parity, 2)
            for h in range(2):
                fold((2 * a + h) * ROWS, slot, 2 * k + h, 1 + a)
        return carry

    lax.fori_loop(0, chunks // 2, near, 0)
    for a in range(answers):
        close(a, 1 + a)

    lens_r.wait()
    set_bias(2, lens[2])
    first = 1 + answers

    def far(i, carry):
        piece(i).wait()
        k, b = i // answers, lax.rem(i, answers)
        rows = pl.ds(pl.multiple_of(k * ROWS, ROWS), ROWS)
        fresh[...] = unit_rows(raw[2, b, rows])
        mine = lax.rem(b + parity, answers)
        for a in range(answers):
            score(fresh[...], answers + a, a * ROWS)
        score(fresh[...], mine, answers * ROWS)
        for a in range(answers):
            fold(a * ROWS, 2 * answers + b, k, first + a * answers + b)
        fold(answers * ROWS, 2 * answers + b, k, first + answers * answers + mine)
        return carry

    lax.fori_loop(0, answers * chunks, far, 0)

    back_r = remote(total.at[pl.ds(2 * answers, answers)], back.at[1], pieces + 3, other)
    back_c = remote(total.at[pl.ds(answers, answers)], back.at[0], pieces + 4, partner)
    for p in range(answers * answers):
        close(answers + p // answers, first + p)
    back_r.start()
    for a in range(answers):
        close(a, first + answers * answers + a)
    back_c.start()
    back_c.wait()
    back_r.wait()
    for a in range(answers):
        whole = total[a] + back[0, a] + back[1, a]
        out_ref[a : a + 1] = jnp.where(bias[a] == 0.0, whole, 0.0)


def solution(mesh):
    n = mesh.shape["cand"]

    def shards(embeddings, lengths):
        answers, length, width = embeddings.shape
        chunks = length // ROWS
        pairs = 1 + 2 * answers + answers * answers
        sums = pl.pallas_call(
            functools.partial(kernel, n),
            out_shape=jax.ShapeDtypeStruct((answers, length), jnp.float32),
            in_specs=[
                pl.BlockSpec(memory_space=pl.ANY),
                pl.BlockSpec(memory_space=pltpu.SMEM),
            ],
            out_specs=pl.BlockSpec(memory_space=pltpu.VMEM),
            scratch_shapes=[
                pltpu.VMEM((3, answers, length, width), jnp.bfloat16),
                pltpu.VMEM((2 * answers, length, width), jnp.bfloat16),
                pltpu.VMEM((2 * answers, width, length), jnp.bfloat16),
                pltpu.VMEM((ROWS, width), jnp.bfloat16),
                pltpu.VMEM((2 * answers * ROWS, length), jnp.float32),
                pltpu.VMEM((3, answers, 128), jnp.int32),
                pltpu.VMEM((3 * answers, 1, length), jnp.float32),
                pltpu.VMEM((pairs, 1, length), jnp.float32),
                pltpu.VMEM((pairs, 1, length), jnp.float32),
                pltpu.VMEM((3 * answers, 1, length), jnp.float32),
                pltpu.VMEM((2, answers, 1, length), jnp.float32),
                pltpu.SemaphoreType.DMA,
                pltpu.SemaphoreType.DMA((answers * chunks + 5,)),
                pltpu.SemaphoreType.DMA((answers * chunks + 5,)),
            ],
            compiler_params=pltpu.CompilerParams(collective_id=0, has_side_effects=True),
            name="consensus",
        )(embeddings, lengths)
        return sums / (answers - 1 + 4 * answers)

    return jax.shard_map(
        shards,
        mesh=mesh,
        in_specs=(P(("group", "cand"), None, None), P(("group", "cand"))),
        out_specs=P(("group", "cand"), None),
        check_vma=False,
    )
```

```python
import functools

import jax
import jax.numpy as jnp
from jax import lax
from jax.experimental import pallas as pl
from jax.experimental.pallas import tpu as pltpu
from jax.sharding import PartitionSpec as P

MESH = pl.DeviceIdType.MESH
INV_TEMP = 256.0
LOW = -1e30
ROWS = 128
WIDE = 256


def unit_rows(raw):
    values = raw.astype(jnp.float32)
    scale = lax.rsqrt(jnp.sum(values * values, axis=-1, keepdims=True) + 1e-06)
    return (values * scale).astype(jnp.bfloat16)


def kernel(
    n, x_hbm, lens_ref, out_ref,
    raw, units, across, fresh, board, lens, bias, peak, mass, total, back,
    local_sem, send_sem, recv_sem,
):
    answers, length = x_hbm.shape[0], x_hbm.shape[1]
    chunks = length // ROWS
    pieces = answers * chunks
    me = lax.axis_index("cand")
    parity = lax.rem(me, 2)
    partner = me + 1 - 2 * parity
    other = lax.rem(me + n - 1 + 2 * parity, n)

    for a in range(answers):
        lens[0, a : a + 1] = jnp.full((1, 128), lens_ref[a], jnp.int32)

    barrier = pltpu.get_barrier_semaphore()
    for device in (partner, other):
        pl.semaphore_signal(barrier, inc=1, device_id={"cand": device}, device_id_type=MESH)
    local = pltpu.make_async_copy(x_hbm, raw.at[0], local_sem)
    local.start()
    pl.semaphore_wait(barrier, 2)

    def remote(src, dst, sem, device):
        return pltpu.make_async_remote_copy(
            src_ref=src, dst_ref=dst, send_sem=send_sem.at[sem], recv_sem=recv_sem.at[sem],
            device_id={"cand": device}, device_id_type=MESH,
        )

    def piece(i):
        b, k = lax.rem(i, answers), i // answers
        rows = pl.ds(pl.multiple_of(k * ROWS, ROWS), ROWS)
        return remote(x_hbm.at[b, rows], raw.at[2, b, rows], i, other)

    lens_c = remote(lens.at[0], lens.at[1], pieces, partner)
    lens_r = remote(lens.at[0], lens.at[2], pieces + 1, other)
    block_c = remote(x_hbm, raw.at[1], pieces + 2, partner)
    lens_r.start()
    lens_c.start()
    block_c.start()

    def launch(i, carry):
        piece(i).start()
        return carry

    lax.fori_loop(0, pieces, launch, 0)

    lane = lax.broadcasted_iota(jnp.int32, (1, length), 1)
    eye = lax.broadcasted_iota(jnp.int32, (ROWS, ROWS), 0) == lax.broadcasted_iota(
        jnp.int32, (ROWS, ROWS), 1
    )
    total[...] = jnp.zeros_like(total)
    peak[...] = jnp.full_like(peak, LOW)
    mass[...] = jnp.zeros_like(mass)

    def set_bias(slot, counts):
        for a in range(answers):
            bias[slot * answers + a] = jnp.where(lane < counts[a : a + 1, 0:1], 0.0, LOW)

    def normalise(slot):
        def one(i, carry):
            a, k = i // chunks, lax.rem(i, chunks)
            rows = pl.ds(pl.multiple_of(k * ROWS, ROWS), ROWS)
            unit = unit_rows(raw[slot, a, rows])
            units[slot * answers + a, rows] = unit
            across[slot * answers + a, :, rows] = unit.T
            return carry

        lax.fori_loop(0, answers * chunks, one, 0)

    def score(query, left, place):
        for j in range(0, length, WIDE):
            board[pl.ds(place, query.shape[0]), j : j + WIDE] = INV_TEMP * lax.dot_general(
                query, across[left, :, j : j + WIDE], (((1,), (0,)), ((), ())),
                preferred_element_type=jnp.float32,
            ) + bias[left, :, j : j + WIDE]

    def fold(tiles, row_slot, k):
        cols = pl.ds(pl.multiple_of(k * ROWS, ROWS), ROWS)
        row_bias = jnp.broadcast_to(bias[row_slot, :, cols], (ROWS, ROWS))
        row_bias = jnp.sum(jnp.where(eye, row_bias, 0.0), axis=1, keepdims=True)
        term = sum(soften(place, row_bias, pair) for place, pair in tiles)
        term = jnp.sum(jnp.where(eye, jnp.broadcast_to(term, (ROWS, ROWS)), 0.0), axis=0, keepdims=True)
        total[row_slot, :, cols] = total[row_slot, :, cols] + term

    def soften(place, row_bias, pair):
        rows = pl.ds(place, ROWS)
        tops = None
        for j in range(0, length, WIDE):
            scores = board[rows, j : j + WIDE] + row_bias
            board[rows, j : j + WIDE] = scores
            before = peak[pair, :, j : j + WIDE]
            now = jnp.maximum(before, jnp.max(scores, axis=0, keepdims=True))
            peak[pair, :, j : j + WIDE] = now
            mass[pair, :, j : j + WIDE] = mass[pair, :, j : j + WIDE] * jnp.exp(
                before - now
            ) + jnp.sum(jnp.exp(scores - now), axis=0, keepdims=True)
            for i in range(0, WIDE, 128):
                part = scores[:, i : i + 128]
                tops = part if tops is None else jnp.maximum(tops, part)
        top = jnp.max(tops, axis=1, keepdims=True)
        sums = None
        for j in range(0, length, 128):
            part = jnp.exp(board[rows, j : j + 128] - top)
            sums = part if sums is None else sums + part
        return (top + jnp.log(jnp.sum(sums, axis=1, keepdims=True))) / INV_TEMP

    def close(left, pair):
        total[left] = total[left] + (peak[pair] + jnp.log(mass[pair])) / INV_TEMP

    local.wait()
    set_bias(0, lens[0])
    normalise(0)

    def own(k, carry):
        rows = pl.ds(pl.multiple_of(k * (2 * ROWS), 2 * ROWS), 2 * ROWS)
        score(units[1, rows], 0, 0)
        for h in range(2):
            fold([(h * ROWS, 0)], 1, 2 * k + h)
        return carry

    lax.fori_loop(0, chunks // 2, own, 0)
    close(0, 0)

    lens_c.wait()
    block_c.wait()
    set_bias(1, lens[1])
    normalise(1)

    def near(k, carry):
        rows = pl.ds(pl.multiple_of(k * (2 * ROWS), 2 * ROWS), 2 * ROWS)
        for a in range(answers):
            slot = answers + lax.rem(a + parity, 2)
            score(units[slot, rows], a, a * 2 * ROWS)
        for a in range(answers):
            slot = answers + lax.rem(a + parity, 2)
            for h in range(2):
                fold([((2 * a + h) * ROWS, 1 + a)], slot, 2 * k + h)
        return carry

    lax.fori_loop(0, chunks // 2, near, 0)
    for a in range(answers):
        close(a, 1 + a)

    lens_r.wait()
    set_bias(2, lens[2])
    first = 1 + answers

    def far(i, carry):
        piece(i).wait()
        k, b = i // answers, lax.rem(i, answers)
        rows = pl.ds(pl.multiple_of(k * ROWS, ROWS), ROWS)
        fresh[...] = unit_rows(raw[2, b, rows])
        mine = lax.rem(b + parity, answers)
        for a in range(answers):
            score(fresh[...], answers + a, a * ROWS)
        score(fresh[...], mine, answers * ROWS)
        tiles = [(a * ROWS, first + a * answers + b) for a in range(answers)]
        tiles.append((answers * ROWS, first + answers * answers + mine))
        fold(tiles, 2 * answers + b, k)
        return carry

    lax.fori_loop(0, answers * chunks, far, 0)

    back_r = remote(total.at[pl.ds(2 * answers, answers)], back.at[1], pieces + 3, other)
    back_c = remote(total.at[pl.ds(answers, answers)], back.at[0], pieces + 4, partner)
    for p in range(answers * answers):
        close(answers + p // answers, first + p)
    back_r.start()
    for a in range(answers):
        close(a, first + answers * answers + a)
    back_c.start()
    back_c.wait()
    back_r.wait()
    for a in range(answers):
        whole = total[a] + back[0, a] + back[1, a]
        out_ref[a : a + 1] = jnp.where(bias[a] == 0.0, whole, 0.0)


def solution(mesh):
    n = mesh.shape["cand"]

    def shards(embeddings, lengths):
        answers, length, width = embeddings.shape
        chunks = length // ROWS
        pairs = 1 + 2 * answers + answers * answers
        sums = pl.pallas_call(
            functools.partial(kernel, n),
            out_shape=jax.ShapeDtypeStruct((answers, length), jnp.float32),
            in_specs=[
                pl.BlockSpec(memory_space=pl.ANY),
                pl.BlockSpec(memory_space=pltpu.SMEM),
            ],
            out_specs=pl.BlockSpec(memory_space=pltpu.VMEM),
            scratch_shapes=[
                pltpu.VMEM((3, answers, length, width), jnp.bfloat16),
                pltpu.VMEM((2 * answers, length, width), jnp.bfloat16),
                pltpu.VMEM((2 * answers, width, length), jnp.bfloat16),
                pltpu.VMEM((ROWS, width), jnp.bfloat16),
                pltpu.VMEM((2 * answers * ROWS, length), jnp.float32),
                pltpu.VMEM((3, answers, 128), jnp.int32),
                pltpu.VMEM((3 * answers, 1, length), jnp.float32),
                pltpu.VMEM((pairs, 1, length), jnp.float32),
                pltpu.VMEM((pairs, 1, length), jnp.float32),
                pltpu.VMEM((3 * answers, 1, length), jnp.float32),
                pltpu.VMEM((2, answers, 1, length), jnp.float32),
                pltpu.SemaphoreType.DMA,
                pltpu.SemaphoreType.DMA((answers * chunks + 5,)),
                pltpu.SemaphoreType.DMA((answers * chunks + 5,)),
            ],
            compiler_params=pltpu.CompilerParams(collective_id=0, has_side_effects=True),
            name="consensus",
        )(embeddings, lengths)
        return sums / (answers - 1 + 4 * answers)

    return jax.shard_map(
        shards,
        mesh=mesh,
        in_specs=(P(("group", "cand"), None, None), P(("group", "cand"))),
        out_specs=P(("group", "cand"), None),
        check_vma=False,
    )
```
